32 devices in a mesh: row: 4 (over z), col: 8 (over y, x, core).
Axes of the slice: x: 2, y: 2, z: 4, core: 2. Of those that a mesh axis runs over, the one named last changes fastest.
Arguments:
- embeddings: bfloat16 [8192, 768], P(('row', 'col'))
- spread: bfloat16 [8192], P(('row', 'col')), may hold values from 1 to 16
- features: bfloat16 [8192, 256], P(('row', 'col')), may hold values from -160 to 160
- block_list: int32 [64], replicated, may hold values from 0 to 63
- list_pairs: int32 [64, 64], replicated, may hold values from 0 to 1, as said below
Outputs:
- smoothed: float32 [8192, 256], P(('row', 'col'))
The draws below stay inside these ranges and needn't reach their ends.
Inputs may be any that keep to these rules, and one draw needn't show every extreme that they name: `list_pairs`: symmetric, with ones on the diagonal.
All inputs are finite; a program needn't handle non-finite values.
Results may differ from the reference program's by a relative error of at most 0.0029.
Values may be sent and summed in bfloat16 or wider, within the bound.
No kernel may reach another device: no remote copies, remote signals or barrier semaphores. Data moves between devices by JAX's collectives and lax.ppermute only.
A program may use at most 64 MiB of HBM per device.

```python
import math
import jax
import jax.numpy as jnp
import numpy as np
from jax import lax

E = 768
F = 256
BLK = 128
LISTS = 64
N = 8192
NB = 64


def draw_embeddings(key, part):
    key_base = jax.random.fold_in(key, 11)
    key_values = jax.random.fold_in(key_base, 0)
    values = jnp.clip(jax.random.normal(key_values, (N, E), jnp.float32), -4.0, 4.0)
    return (values / jnp.sqrt(jnp.float32(E))).astype(jnp.bfloat16)


def draw_list_pairs(key, part):
    key_base = jax.random.fold_in(key, 23)
    picks = (jax.random.randint(key_base, (LISTS, LISTS), 0, 4) == 0).astype(jnp.int32)
    upper = jnp.triu(picks, 1)
    table = upper + upper.T + jnp.eye(LISTS, dtype=jnp.int32)
    return table.astype(jnp.int32)


def plant(entries, stream_key, low, largest):
    longest = entries.shape.index(max(entries.shape))
    spots = []
    for shift in (0, 1):
        where = [jax.random.randint(jax.random.fold_in(stream_key, axis), (), 0, length) for axis, length in enumerate(entries.shape)]
        where[longest] = (where[longest] + shift) % entries.shape[longest]
        spots.append(tuple(where))
    return entries.at[spots[0]].set(low).at[spots[1]].set(largest)


def block_scale(key, shape, cuts, smallest, largest):
    def one(axis_at, blocks):
        heights = jax.random.uniform(jax.random.fold_in(jax.random.fold_in(key, 6), axis_at), (blocks,), jnp.float32, smallest / len(cuts), largest / len(cuts))
        return jnp.repeat(jnp.exp(heights), shape[axis_at] // blocks).reshape((-1,) + (1,) * (len(shape) - axis_at - 1))

    level = one(*cuts[0])
    for cut in cuts[1:]:
        level = level * one(*cut)
    return level


def rank_bounds(amount, lean):
    weights = [(1 << 20) // math.isqrt(grade ** lean) + 1 for grade in range(1, amount + 1)]
    width = 1 + sum(weights) // (1 << 30)
    return np.cumsum(np.array([max(1, weight // width) for weight in weights]))


def skewed_ids(stream_key, shape, amount, skew):
    grid = rank_bounds(amount, skew)
    pick = jax.random.randint(jax.random.fold_in(stream_key, 1), shape, 0, int(grid[amount - 1]))
    standing = jnp.searchsorted(jnp.asarray(grid, jnp.int32), pick, side="right")
    return jax.random.permutation(jax.random.fold_in(stream_key, 2), amount)[standing].astype(jnp.int32)


def normal_values(own_key, dims, scale, most, pieces=(), held_as=jnp.bfloat16):
    result = jax.random.normal(own_key, dims, jnp.float32) * scale
    if len(pieces) > 0:
        result = block_scale(own_key, dims, pieces, -0.22, 0.18) * result
    return jnp.clip(result, min=-most, max=most).astype(held_as)


def setup_inputs(seed: int = 0) -> dict:
    keys = jax.random.split(jax.random.key(seed), 6)
    embeddings = draw_embeddings(jax.random.fold_in(keys[5], 71), 0)
    spread = jnp.clip(jnp.exp(math.log(16.0) - 2.7725887 * jax.random.uniform(keys[1], (N,), jnp.float32) ** block_scale(keys[1], (N,), ((0, 32),), -0.2, 0.2)), 1.0, 16.0).astype(jnp.bfloat16)
    features = normal_values(keys[2], (N, F), 32.0, 160.0, ((0, 32),))
    block_list = plant(skewed_ids(keys[3], (NB,), LISTS, 2), jax.random.fold_in(keys[3], 3), 0, LISTS - 1).astype(jnp.int32)
    list_pairs = draw_list_pairs(jax.random.fold_in(keys[5], 71), 0)
    return dict(embeddings=embeddings, spread=spread, features=features, block_list=block_list, list_pairs=list_pairs)


def active_table(block_list, list_pairs, row_blocks, col_blocks):
    count = block_list.shape[0]
    lists_onehot = (block_list[:, None] == jnp.arange(LISTS, dtype=jnp.int32)[None, :]).astype(jnp.float32)
    pair_table = list_pairs.astype(jnp.float32)
    row_select = (row_blocks[:, None] == jnp.arange(count, dtype=jnp.int32)[None, :]).astype(jnp.float32)
    col_select = (col_blocks[:, None] == jnp.arange(count, dtype=jnp.int32)[None, :]).astype(jnp.float32)
    row_onehot = jnp.dot(row_select, lists_onehot, precision=lax.Precision.HIGHEST)
    col_onehot = jnp.dot(col_select, lists_onehot, precision=lax.Precision.HIGHEST)
    joined = jnp.dot(row_onehot, pair_table, precision=lax.Precision.HIGHEST)
    return jnp.dot(joined, col_onehot.T, precision=lax.Precision.HIGHEST)


def keep_mask(active, row_ids, col_ids):
    size_rows = row_ids.shape[0]
    col_blocks = active.shape[1]
    expanded = jnp.broadcast_to(active[:, None, :, None], (size_rows // BLK, BLK, col_blocks, BLK))
    expanded = expanded.reshape(size_rows, col_blocks * BLK)
    return expanded * (row_ids[:, None] != col_ids[None, :]).astype(jnp.float32)


def reference(embeddings, spread, features, block_list, list_pairs):
    total = embeddings.shape[0]
    block_rows = math.gcd(total, 512)
    norms = jnp.sum(jnp.square(embeddings.astype(jnp.float32)), axis=1)
    beta = spread.astype(jnp.float32)
    all_ids = jnp.arange(total, dtype=jnp.int32)

    def block_terms(start):
        row_emb = lax.dynamic_slice_in_dim(embeddings, start, block_rows, 0)
        row_norm = lax.dynamic_slice_in_dim(norms, start, block_rows, 0)
        row_beta = lax.dynamic_slice_in_dim(beta, start, block_rows, 0)
        inner = lax.dot_general(row_emb, embeddings, (((1,), (1,)), ((), ())), preferred_element_type=jnp.float32)
        dist = row_norm[:, None] + norms[None, :] - 2.0 * inner
        row_ids = start + jnp.arange(block_rows, dtype=jnp.int32)
        active = active_table(block_list, list_pairs, row_ids[::BLK] // BLK, all_ids[::BLK] // BLK)
        mask = keep_mask(active, row_ids, all_ids)
        near = mask * jnp.exp(-row_beta[:, None] * dist)
        far = mask * jnp.exp(-beta[None, :] * dist)
        return near, far, start

    starts = jnp.arange(total // block_rows, dtype=jnp.int32) * block_rows
    row_totals = lax.map(lambda start: jnp.sum(block_terms(start)[0], axis=1), starts).reshape(total)

    def weighted(start):
        near, far, begin = block_terms(start)
        row_total = lax.dynamic_slice_in_dim(row_totals, begin, block_rows, 0)
        weight = ((near / row_total[:, None] + far / row_totals[None, :]) * 0.5).astype(jnp.bfloat16)
        return jnp.dot(weight, features, preferred_element_type=jnp.float32)

    return lax.map(weighted, starts).reshape(total, features.shape[1])
```

```python
import functools
import math

import jax
import jax.numpy as jnp
from jax import lax
from jax.experimental import pallas as pl
from jax.experimental.pallas import tpu as pltpu
from jax.sharding import PartitionSpec as P

BLK = 128
AUX = 8
AXES = ("row", "col")
LOG2E = math.log2(math.e)
FAR_AWAY = 1e37
VMEM = pl.BlockSpec(memory_space=pltpu.VMEM)
SMEM = pl.BlockSpec(memory_space=pltpu.SMEM)


def bits_of(size):
    return [1 << k for k in reversed(range(size.bit_length() - 1))]


def groups(row_size, col_size):
    high = [bit * col_size for bit in bits_of(row_size)]
    low = bits_of(col_size)
    core, low = low[-1:], low[:-1]
    if len(high) > 1:
        high[0] |= high[1]
    cut, mid = len(high) // 2, len(low) // 2
    return high[cut:] + low[:mid] + core, high[:cut] + low[mid:]


def span(bits):
    masks = [0]
    for bit in bits:
        masks += [mask ^ bit for mask in masks]
    return masks


def swap(value, mask, count):
    return lax.ppermute(value, AXES, [(i, i ^ mask) for i in range(count)])


def gather(value, bits, count):
    held = [value]
    for bit in bits:
        held += [swap(one, bit, count) for one in held]
    return held


def packet_kernel(x_ref, spread_ref, out_ref):
    own, width = x_ref.shape
    out_ref[0:own, :] = x_ref[...]
    values = x_ref[...].astype(jnp.float32)
    squares = values * values
    part = squares[:, 0:BLK]
    for start in range(BLK, width, BLK):
        part = part + squares[:, start : start + BLK]
    norm = jnp.sum(part.T, axis=0, keepdims=True)
    first = norm.astype(jnp.bfloat16)
    rest = norm - first.astype(jnp.float32)
    second = rest.astype(jnp.bfloat16)
    third = (rest - second.astype(jnp.float32)).astype(jnp.bfloat16)
    lane = [v.astype(jnp.float32) for v in (first, second, third)]
    spread = spread_ref[...].astype(jnp.float32)
    line = lax.broadcasted_iota(jnp.int32, (AUX, own), 0)
    aux = jnp.zeros((AUX, own), jnp.float32)
    for k, v in enumerate(lane + [spread]):
        aux = jnp.where(line == k, jnp.broadcast_to(v, (AUX, own)), aux)
    out_ref[own : own + AUX, 0:own] = aux.astype(jnp.bfloat16)
    out_ref[own : own + AUX, own:] = jnp.zeros((AUX, width - own), jnp.bfloat16)


def read_aux(ref, own):
    aux = ref[own : own + AUX, 0:own].astype(jnp.float32)
    norm = (aux[0:1] + aux[1:2]) + aux[2:3]
    return norm, aux[3:4] * (-LOG2E)


def down(line):
    return jnp.broadcast_to(line, (BLK, BLK)).T


def near_kernel(row_masks, col_mask, first, last, *refs):
    count = len(row_masks)
    me_ref, list_ref, pair_ref = refs[:3]
    rows, col_ref = refs[3 : 3 + count], refs[3 + count]
    refs = refs[4 + count :]
    if first:
        dist_ref, csum_ref, cbeta_ref, norm_ref, beta_ref, rsum_ref = refs[:6]
        refs = refs[6:]
    else:
        norm_ref, beta_ref, rin_ref, dist_ref, csum_ref, cbeta_ref, rsum_ref = refs[:7]
        refs = refs[7:]
    (twice_ref, racc_ref) = refs
    own = col_ref.shape[0] - AUX
    blocks = own // BLK
    me = me_ref[0]
    twice_ref[...] = col_ref[0:own, :] * 2
    col_norm, col_beta = read_aux(col_ref, own)
    cbeta_ref[...] = jnp.broadcast_to(col_beta, cbeta_ref.shape)
    csum_ref[...] = jnp.zeros_like(csum_ref)
    col_lists = [list_ref[(me ^ col_mask) * blocks + k] for k in range(blocks)]
    lane = lax.broadcasted_iota(jnp.int32, (1, own), 1)

    for slot, row_mask in enumerate(row_masks):
        if first:
            row_norm, row_beta = read_aux(rows[slot], own)
            for b in range(blocks):
                norm_ref[slot * blocks + b] = down(row_norm[:, b * BLK : (b + 1) * BLK])
                beta_ref[slot * blocks + b] = down(row_beta[:, b * BLK : (b + 1) * BLK])

        @pl.loop(0, blocks)
        def _(b, slot=slot, row_mask=row_mask):
            at = slot * blocks + b
            row_list = list_ref[(me ^ row_mask) * blocks + b]
            flags = [pair_ref[row_list, one] for one in col_lists]
            racc_ref[...] = jnp.zeros_like(racc_ref) if first else rin_ref[at]

            @pl.when(functools.reduce(jnp.maximum, flags) > 0)
            def _():
                x = rows[slot][pl.ds(pl.multiple_of(b * BLK, BLK), BLK), :]
                inner = lax.dot_general(
                    x,
                    twice_ref[...],
                    (((1,), (1,)), ((), ())),
                    preferred_element_type=jnp.float32,
                )
                active = jnp.zeros((1, own), jnp.int32)
                for k, flag in enumerate(flags):
                    active = jnp.where(lane // BLK == k, flag, active)
                row_norm, row_beta = norm_ref[at], beta_ref[at]
                for k in range(blocks):
                    cut = slice(k * BLK, (k + 1) * BLK)
                    dist = (row_norm + col_norm[:, cut]) - inner[:, cut]
                    keep = jnp.broadcast_to(active[:, cut], (BLK, BLK)) > 0
                    if row_mask == col_mask:
                        i = lax.broadcasted_iota(jnp.int32, (BLK, BLK), 0)
                        j = lax.broadcasted_iota(jnp.int32, (BLK, BLK), 1)
                        keep = keep & ((i + b * BLK) != (j + k * BLK))
                    dist = jnp.where(keep, dist, FAR_AWAY)
                    dist_ref[at, :, cut] = dist
                    racc_ref[...] += jnp.exp2(row_beta * dist)
                    far = jnp.exp2(col_beta[:, cut] * dist)
                    csum_ref[:, cut] += jnp.sum(far.reshape(BLK // 8, 8, BLK), axis=0)

            if last:
                rsum_ref[pl.ds(at, 1), :] = jnp.sum(racc_ref[...].T, axis=0, keepdims=True)
            else:
                rsum_ref[at] = racc_ref[...]


def weight_kernel(row_masks, col_masks, *refs):
    cols = len(col_masks)
    me_ref, list_ref, pair_ref, beta_ref, rtot_ref, ctot_ref = refs[:6]
    dists, cbetas, feats = (refs[6 + k * cols : 6 + (k + 1) * cols] for k in range(3))
    keep_ref, send_ref, acc_ref = refs[6 + 3 * cols :]
    own = feats[0].shape[0]
    blocks = own // BLK
    half = len(row_masks) // 2
    me = me_ref[0]
    for slot, row_mask in enumerate(row_masks):

        @pl.loop(0, blocks)
        def _(b, slot=slot, row_mask=row_mask):
            at = slot * blocks + b
            row_list = list_ref[(me ^ row_mask) * blocks + b]
            acc_ref[...] = jnp.zeros_like(acc_ref)
            row_scale = down(0.5 / rtot_ref[pl.ds(at, 1), :])
            row_beta = beta_ref[at]
            for c, col_mask in enumerate(col_masks):
                flags = [
                    pair_ref[row_list, list_ref[(me ^ col_mask) * blocks + k]]
                    for k in range(blocks)
                ]

                @pl.when(functools.reduce(jnp.maximum, flags) > 0)
                def _(c=c):
                    parts = []
                    for k in range(blocks):
                        cut = slice(k * BLK, (k + 1) * BLK)
                        dist = dists[c][at, :, cut]
                        near = jnp.exp2(row_beta * dist)
                        far = jnp.exp2(cbetas[c][0:1, cut] * dist)
                        col_scale = 0.5 / ctot_ref[c : c + 1, cut]
                        parts.append((near * row_scale + far * col_scale).astype(jnp.bfloat16))
                    acc_ref[...] += jnp.dot(
                        jnp.concatenate(parts, axis=1),
                        feats[c][...],
                        preferred_element_type=jnp.float32,
                    )

            place = pl.ds(pl.multiple_of(b * BLK, BLK), BLK)
            if slot < half:
                keep_ref[slot, place, :] = acc_ref[...]
            else:
                send_ref[slot - half, place, :] = acc_ref[...].astype(jnp.bfloat16)


def shards(row_size, col_size, embeddings, spread, features, block_list, list_pairs):
    count = row_size * col_size
    own, width = embeddings.shape
    feat = features.shape[1]
    blocks = own // BLK
    row_bits, col_bits = groups(row_size, col_size)
    row_masks, col_masks = span(row_bits), span(col_bits)
    rows, cols = len(row_masks), len(col_masks)
    me = (lax.axis_index("row") * col_size + lax.axis_index("col")).astype(jnp.int32).reshape(1)
    f32 = functools.partial(jax.ShapeDtypeStruct, dtype=jnp.float32)
    bf16 = functools.partial(jax.ShapeDtypeStruct, dtype=jnp.bfloat16)

    packet = pl.pallas_call(
        packet_kernel,
        out_shape=bf16((own + AUX, width)),
        in_specs=[VMEM, VMEM],
        out_specs=VMEM,
    )(embeddings, spread.reshape(1, own))
    col_packets = gather(packet, col_bits, count)
    row_packets = gather(packet, row_bits, count)
    feats = gather(features, col_bits, count)

    dists, csums, cbetas = [], [], []
    state = None
    for c, col_mask in enumerate(col_masks):
        first, last = c == 0, c == cols - 1
        outs = [f32((rows * blocks, BLK, own)), f32((8, own)), f32((8, own))]
        if first:
            outs += [f32((rows * blocks, BLK, BLK))] * 2
        outs += [f32((rows * blocks, BLK) if last else (rows * blocks, BLK, BLK))]
        args = [*row_packets, col_packets[c]] + ([] if first else list(state))
        work = rows * own * own
        results = pl.pallas_call(
            functools.partial(near_kernel, row_masks, col_mask, first, last),
            out_shape=outs,
            in_specs=[SMEM] * 3 + [VMEM] * len(args),
            out_specs=[VMEM] * len(outs),
            scratch_shapes=[
                pltpu.VMEM((own, width), jnp.bfloat16),
                pltpu.VMEM((BLK, BLK), jnp.float32),
            ],
            cost_estimate=pl.CostEstimate(
                flops=2 * work * width, bytes_accessed=4 * work, transcendentals=2 * work
            ),
        )(me, block_list, list_pairs, *args)
        dists.append(results[0])
        csums.append(results[1])
        cbetas.append(results[2])
        if first:
            norm_rows, beta_rows, racc = results[3:]
        else:
            racc = results[3]
        state = (norm_rows, beta_rows, racc)

    row_total = racc.reshape(rows, own)
    for bit in reversed(row_bits):
        got = swap(row_total, bit, count)
        order = [row_masks.index(mask ^ bit) for mask in row_masks]
        row_total = row_total + jnp.concatenate([got[k : k + 1] for k in order], axis=0)
    col_total = jnp.stack([jnp.sum(one, axis=0) for one in csums])
    for bit in reversed(col_bits):
        got = swap(col_total, bit, count)
        order = [col_masks.index(mask ^ bit) for mask in col_masks]
        col_total = col_total + jnp.concatenate([got[k : k + 1] for k in order], axis=0)

    half = rows // 2
    keep, send = pl.pallas_call(
        functools.partial(weight_kernel, row_masks, col_masks),
        out_shape=[f32((half, own, feat)), bf16((half, own, feat))],
        in_specs=[SMEM] * 3 + [VMEM] * (3 + 3 * cols),
        out_specs=[VMEM] * 2,
        scratch_shapes=[pltpu.VMEM((BLK, feat), jnp.float32)],
    )(
        me,
        block_list,
        list_pairs,
        beta_rows,
        row_total.reshape(rows * blocks, BLK),
        col_total,
        *dists,
        *cbetas,
        *feats,
    )
    got = swap(send, row_bits[-1], count)
    parts = [keep[k] + got[k].astype(jnp.float32) for k in range(half)]
    back = [
        swap(parts[k].astype(jnp.bfloat16), row_masks[k], count).astype(jnp.float32)
        for k in range(1, half)
    ]
    return functools.reduce(jnp.add, back, parts[0])


def solution(mesh):
    return jax.shard_map(
        functools.partial(shards, mesh.shape["row"], mesh.shape["col"]),
        mesh=mesh,
        in_specs=(P(AXES, None), P(AXES), P(AXES, None), P(), P()),
        out_specs=P(AXES, None),
        check_vma=False,
    )
```

```python
import functools
import math

import jax
import jax.numpy as jnp
from jax import lax
from jax.experimental import pallas as pl
from jax.experimental.pallas import tpu as pltpu
from jax.sharding import PartitionSpec as P

BLK = 128
AUX = 8
AXES = ("row", "col")
LOG2E = math.log2(math.e)
FAR_AWAY = 1e37
VMEM = pl.BlockSpec(memory_space=pltpu.VMEM)
SMEM = pl.BlockSpec(memory_space=pltpu.SMEM)


def bits_of(size):
    return [1 << k for k in reversed(range(size.bit_length() - 1))]


def groups(row_size, col_size):
    high = [bit * col_size for bit in bits_of(row_size)]
    low = bits_of(col_size)
    core, low = low[-1:], low[:-1]
    if len(high) > 1:
        high[0] |= high[1]
    cut, mid = len(high) // 2, len(low) // 2
    return high[cut:] + low[:mid] + core, high[:cut] + low[mid:]


def span(bits):
    masks = [0]
    for bit in bits:
        masks += [mask ^ bit for mask in masks]
    return masks


def swap(value, mask, count):
    return lax.ppermute(value, AXES, [(i, i ^ mask) for i in range(count)])


def gather(value, bits, count):
    held = [value]
    for bit in bits:
        held += [swap(one, bit, count) for one in held]
    return held


def packet_kernel(x_ref, spread_ref, out_ref):
    own, width = x_ref.shape
    out_ref[0:own, :] = x_ref[...]
    values = x_ref[...].astype(jnp.float32)
    squares = values * values
    part = squares[:, 0:BLK]
    for start in range(BLK, width, BLK):
        part = part + squares[:, start : start + BLK]
    norm = jnp.sum(part.T, axis=0, keepdims=True)
    first = norm.astype(jnp.bfloat16)
    rest = norm - first.astype(jnp.float32)
    second = rest.astype(jnp.bfloat16)
    third = (rest - second.astype(jnp.float32)).astype(jnp.bfloat16)
    lane = [v.astype(jnp.float32) for v in (first, second, third)]
    spread = spread_ref[...].astype(jnp.float32)
    line = lax.broadcasted_iota(jnp.int32, (AUX, own), 0)
    aux = jnp.zeros((AUX, own), jnp.float32)
    for k, v in enumerate(lane + [spread]):
        aux = jnp.where(line == k, jnp.broadcast_to(v, (AUX, own)), aux)
    out_ref[own : own + AUX, 0:own] = aux.astype(jnp.bfloat16)
    out_ref[own : own + AUX, own:] = jnp.zeros((AUX, width - own), jnp.bfloat16)


def read_aux(ref, own):
    aux = ref[own : own + AUX, 0:own].astype(jnp.float32)
    norm = (aux[0:1] + aux[1:2]) + aux[2:3]
    return norm, aux[3:4] * (-LOG2E)


def down(line):
    return jnp.broadcast_to(line, (BLK, BLK)).T


def plan_kernel(row_masks, col_masks, calls, blocks, *refs):
    me_ref, list_ref, pair_ref, code_ref, size_ref = refs
    me = me_ref[0]
    wide = len(col_masks) * blocks
    room = code_ref.shape[0] // len(calls)
    row_lists = [list_ref[(me ^ mask) * blocks + b] for mask in row_masks for b in range(blocks)]
    col_lists = [list_ref[(me ^ mask) * blocks + b] for mask in col_masks for b in range(blocks)]
    for g, slots in enumerate(calls):
        size = jnp.int32(g * room)
        if g == 0:
            for b in range(blocks):
                code_ref[b] = b * wide + b
            size = jnp.int32(blocks)
        for r, row_list in enumerate(row_lists):
            for c in range(slots[0] * blocks, (slots[-1] + 1) * blocks):
                if g > 0 or r != c or r >= blocks:
                    code_ref[size] = r * wide + c
                    size = size + pair_ref[row_list, col_lists[c]]
        code_ref[size] = slots[0] * blocks
        size_ref[g] = size - g * room


def near_kernel(own, wide, group, room, slots, first, last, *refs):
    blocks = own // BLK
    base, part = slots[0] * blocks, len(slots) * blocks
    refs = list(refs)
    take = lambda n: [refs.pop(0) for _ in range(n)]
    code_ref, size_ref = take(2)
    cols = take(len(slots))
    if first:
        rows = take((len(refs) - 9))
    else:
        x_ref, norm_ref, beta_ref, rin_ref = take(4)
    dist_ref, csum_ref, cbeta_ref, racc_ref = take(4)
    if first:
        x_ref, norm_ref, beta_ref = take(3)
    if last:
        (rsum_ref,) = take(1)
    twice_ref, cnorm_ref = take(2)

    for s, col_ref in enumerate(cols):
        col_norm, col_beta = read_aux(col_ref, own)
        for k in range(blocks):
            cut = slice(k * BLK, (k + 1) * BLK)
            twice_ref[s * blocks + k] = col_ref[cut, :] * 2
            cnorm_ref[s * blocks + k] = jnp.broadcast_to(col_norm[:, cut], (8, BLK))
            cbeta_ref[s * blocks + k] = jnp.broadcast_to(col_beta[:, cut], (8, BLK))
    csum_ref[...] = jnp.zeros_like(csum_ref)
    if first:
        racc_ref[...] = jnp.zeros_like(racc_ref)
        for slot, row_ref in enumerate(rows):
            row_norm, row_beta = read_aux(row_ref, own)
            for b in range(blocks):
                cut = slice(b * BLK, (b + 1) * BLK)
                x_ref[slot * blocks + b] = row_ref[cut, :]
                norm_ref[slot * blocks + b] = down(row_norm[:, cut])
                beta_ref[slot * blocks + b] = down(row_beta[:, cut])
    else:
        racc_ref[...] = rin_ref[...]

    def decode(k):
        code = code_ref[group * room + k]
        return code // wide, code % wide - base

    def product(at, c):
        return lax.dot_general(
            x_ref[at], twice_ref[c], (((1,), (1,)), ((), ())), preferred_element_type=jnp.float32
        )

    def spend(at, c, inner, keep=None):
        dist = (norm_ref[at] + cnorm_ref[c, 0:1, :]) - inner
        if keep is not None:
            dist = jnp.where(keep, dist, FAR_AWAY)
        dist_ref[at * part + c] = dist
        racc_ref[at] += jnp.exp2(beta_ref[at] * dist)
        far = jnp.exp2(cbeta_ref[c, 0:1, :] * dist)
        csum_ref[c] += jnp.sum(far.reshape(BLK // 8, 8, BLK), axis=0)

    start = 0
    if first:
        start = blocks
        i = lax.broadcasted_iota(jnp.int32, (BLK, BLK), 0)
        j = lax.broadcasted_iota(jnp.int32, (BLK, BLK), 1)
        for b in range(blocks):
            spend(b, b, product(b, b), i != j)

    def step(k, inner):
        ahead = product(*decode(k + 1))
        spend(*decode(k), inner)
        return ahead

    lax.fori_loop(start, size_ref[group], step, product(*decode(start)))
    if last:
        for at in range(racc_ref.shape[0]):
            rsum_ref[at : at + 1, :] = jnp.sum(racc_ref[at].T, axis=0, keepdims=True)


def weight_kernel(own, calls, room, *refs):
    blocks = own // BLK
    cols = calls[-1][-1] + 1
    wide = cols * blocks
    refs = list(refs)
    take = lambda n: [refs.pop(0) for _ in range(n)]
    code_ref, size_ref, beta_ref, rtot_ref, ctot_ref = take(5)
    dists, cbetas, feats = take(len(calls)), take(len(calls)), take(cols)
    keep_ref, send_ref, acc_ref, scale_ref, cscale_ref, feat_ref = refs
    for c in range(cols):
        for k in range(blocks):
            cut = slice(k * BLK, (k + 1) * BLK)
            feat_ref[c * blocks + k] = feats[c][cut, :]
            cscale_ref[c * blocks + k] = jnp.broadcast_to(0.5 / ctot_ref[c : c + 1, cut], (8, BLK))
    acc_ref[...] = jnp.zeros_like(acc_ref)
    for at in range(scale_ref.shape[0]):
        scale_ref[at] = down(0.5 / rtot_ref[at : at + 1, :])

    for g, slots in enumerate(calls):
        base, part = slots[0] * blocks, len(slots) * blocks

        def decode(k, g=g):
            code = code_ref[g * room + k]
            return code // wide, code % wide

        def apply(k, weight, decode=decode):
            at, c = decode(k)
            acc_ref[at] += jnp.dot(weight, feat_ref[c], preferred_element_type=jnp.float32)

        def step(k, weight, g=g, base=base, part=part, decode=decode, apply=apply):
            apply(jnp.maximum(k - 1, 0), weight)
            at, c = decode(k)
            dist = dists[g][at * part + c - base]
            near = jnp.exp2(beta_ref[at] * dist) * scale_ref[at]
            far = jnp.exp2(cbetas[g][c - base, 0:1, :] * dist) * cscale_ref[c, 0:1, :]
            return (near + far).astype(jnp.bfloat16)

        size = size_ref[g]
        weight = lax.fori_loop(0, size, step, jnp.zeros((BLK, BLK), jnp.bfloat16))
        apply(jnp.maximum(size - 1, 0), weight)

    half = keep_ref.shape[0]
    for slot in range(half):
        for b in range(blocks):
            cut = slice(b * BLK, (b + 1) * BLK)
            keep_ref[slot, cut, :] = acc_ref[slot * blocks + b]
            send_ref[slot, cut, :] = acc_ref[(half + slot) * blocks + b].astype(jnp.bfloat16)


def shards(row_size, col_size, embeddings, spread, features, block_list, list_pairs):
    count = row_size * col_size
    own, width = embeddings.shape
    feat = features.shape[1]
    blocks = own // BLK
    row_bits, col_bits = groups(row_size, col_size)
    row_masks, col_masks = span(row_bits), span(col_bits[1:])
    early = len(col_masks)
    col_masks = col_masks + [mask ^ col_bits[0] for mask in col_masks]
    rows, cols = len(row_masks), len(col_masks)
    calls = [list(range(early)), list(range(early, cols - 1)), [cols - 1]]
    calls = [slots for slots in calls if slots]
    tall, wide = rows * blocks, cols * blocks
    room = tall * early * blocks + 8
    me = (lax.axis_index("row") * col_size + lax.axis_index("col")).astype(jnp.int32).reshape(1)
    f32 = functools.partial(jax.ShapeDtypeStruct, dtype=jnp.float32)
    bf16 = functools.partial(jax.ShapeDtypeStruct, dtype=jnp.bfloat16)

    def kernel(body, outs, scratch, *args, smem=0, smem_out=False, **more):
        size = sum(math.prod(a.shape) * a.dtype.itemsize for a in [*args, *outs, *scratch])
        return pl.pallas_call(
            body,
            out_shape=outs,
            in_specs=[SMEM] * smem + [VMEM] * (len(args) - smem),
            out_specs=[SMEM if smem_out else VMEM] * len(outs),
            scratch_shapes=[pltpu.VMEM(a.shape, a.dtype) for a in scratch],
            compiler_params=pltpu.CompilerParams(vmem_limit_bytes=size + (2 << 20)),
            **more,
        )(*args)

    (packet,) = kernel(packet_kernel, [bf16((own + AUX, width))], [], embeddings, spread)

    def reach(value, masks, bits):
        held = dict(zip(span(bits), gather(value, bits, count)))
        return [held[mask] for mask in masks]

    col_packets = reach(packet, col_masks, col_bits)
    row_packets = reach(packet, row_masks, row_bits)
    feats = reach(features, col_masks, col_bits)
    code, size = kernel(
        functools.partial(plan_kernel, row_masks, col_masks, calls, blocks),
        [jax.ShapeDtypeStruct((n,), jnp.int32) for n in (len(calls) * room, len(calls))],
        [],
        me,
        block_list,
        list_pairs,
        smem=3,
        smem_out=True,
    )

    dists, csums, cbetas = [], [], []
    for g, slots in enumerate(calls):
        first, last = g == 0, g == len(calls) - 1
        part = len(slots) * blocks
        outs = [f32((tall * part, BLK, BLK)), f32((part, 8, BLK)), f32((part, 8, BLK))]
        outs += [f32((tall, BLK, BLK))]
        if first:
            outs += [bf16((tall, BLK, width))] + [f32((tall, BLK, BLK))] * 2
        if last:
            outs += [f32((tall, BLK))]
        work = tall * part * BLK * BLK // 3
        results = kernel(
            functools.partial(near_kernel, own, wide, g, room, slots, first, last),
            outs,
            [bf16((part, BLK, width)), f32((part, 8, BLK))],
            code,
            size,
            *[col_packets[c] for c in slots],
            *(row_packets if first else state),
            smem=2,
            cost_estimate=pl.CostEstimate(
                flops=2 * work * width, bytes_accessed=4 * work, transcendentals=2 * work
            ),
        )
        dists.append(results[0])
        csums.append(results[1])
        cbetas.append(results[2])
        if first:
            x_rows, norm_rows, beta_rows = results[4:7]
        state = (x_rows, norm_rows, beta_rows, results[3])

    row_total = results[4].reshape(rows, own)
    for bit in reversed(row_bits):
        got = swap(row_total, bit, count)
        order = [row_masks.index(mask ^ bit) for mask in row_masks]
        row_total = row_total + jnp.concatenate([got[k : k + 1] for k in order], axis=0)
    col_total = jnp.concatenate([jnp.sum(one, axis=1) for one in csums]).reshape(cols, own)
    for bit in reversed(col_bits):
        got = swap(col_total, bit, count)
        order = [col_masks.index(mask ^ bit) for mask in col_masks]
        col_total = col_total + jnp.concatenate([got[k : k + 1] for k in order], axis=0)

    half = rows // 2
    keep, send = kernel(
        functools.partial(weight_kernel, own, calls, room),
        [f32((half, own, feat)), bf16((half, own, feat))],
        [
            f32((tall, BLK, feat)),
            f32((tall, BLK, BLK)),
            f32((wide, 8, BLK)),
            bf16((wide, BLK, feat)),
        ],
        code,
        size,
        beta_rows,
        row_total.reshape(tall, BLK),
        col_total,
        *dists,
        *cbetas,
        *feats,
        smem=2,
    )
    got = swap(send, row_bits[-1], count)
    parts = [keep[k] + got[k].astype(jnp.float32) for k in range(half)]
    back = [
        swap(parts[k].astype(jnp.bfloat16), row_masks[k], count).astype(jnp.float32)
        for k in range(1, half)
    ]
    return functools.reduce(jnp.add, back, parts[0])


def solution(mesh):
    return jax.shard_map(
        functools.partial(shards, mesh.shape["row"], mesh.shape["col"]),
        mesh=mesh,
        in_specs=(P(AXES, None), P(AXES), P(AXES, None), P(), P()),
        out_specs=P(AXES, None),
        check_vma=False,
    )
```
